32 devices in a mesh: sector: 4 (over z), group: 8 (over y, x, core).
Axes of the slice: x: 2, y: 2, z: 4, core: 2. Of those that a mesh axis runs over, the one named last changes fastest.
Arguments:
- spectrum: float32 [1152, 128, 512], P('group', None, 'sector'), may hold values from 0.1 to 2
- land_mask: int32 [128, 512], P(None, 'sector'), may hold values 0 or 1
- wind_field: float32 [2, 128, 512], P(None, 'group', 'sector'), may hold values from -3 to 3
- assignment: int32 [1152], replicated, may hold values from 0 to 1151, each once
- courant: float32 [32], replicated, may hold values from 0.3 to 0.65
- growth: float32 [32], replicated, may hold values from 0.1 to 0.5
- whitecap: float32 [32], replicated, may hold values from 0.2 to 1
- weights: float32 [32], replicated, may hold values from 0.5 to 5
- spread: float32 [32, 36, 36], replicated, may hold values from -1 to 1
Outputs:
- updated: float32 [1152, 128, 512], P('group', None, 'sector')
The draws below stay inside these ranges and needn't reach their ends.
Inputs may be any that keep to these rules, and one draw needn't show every extreme that they name: `assignment`: each component number appears exactly once.
All inputs are finite; a program needn't handle non-finite values. No bound on the sum of `land_mask` on one device may be relied on, other than what follows from the above.
Results may differ from the reference program's by a relative error of at most 0.00007.
Values sent between devices are 32-bit elements; how exact they have to be, the bound alone decides.
No kernel may reach another device: no remote copies, remote signals or barrier semaphores. Data moves between devices by JAX's collectives and lax.ppermute only.
A program may use at most 128 MiB of HBM per device.

```python
import math
import jax
import jax.numpy as jnp
from jax import lax

DIRS = 36
FREQ = 32
SUBSTEPS = 6
LAT = 128
COMPS = 1152
LON = 512


def touch_ends(entries, rng, smallest, top_value):
    longest = entries.shape.index(max(entries.shape))
    spots = []
    for shift in (0, 1):
        where = [jax.random.randint(jax.random.fold_in(rng, axis), (), 0, length) for axis, length in enumerate(entries.shape)]
        where[longest] = (where[longest] + shift) % entries.shape[longest]
        spots.append(tuple(where))
    return entries.at[spots[0]].set(smallest).at[spots[1]].set(top_value)


def block_levels(key, dims, cuts, low, largest):
    def one(axis_at, shards_of):
        heights = jax.random.uniform(jax.random.fold_in(jax.random.fold_in(key, 6), axis_at), (shards_of,), jnp.float32, low / len(cuts), largest / len(cuts))
        return jnp.repeat(jnp.exp(heights), dims[axis_at] // shards_of).reshape((-1,) + (1,) * (len(dims) - axis_at - 1))

    gain = one(*cuts[0])
    for cut in cuts[1:]:
        gain = gain * one(*cut)
    return gain


def noise(key, shape, width, most, cuts=(), dtype=jnp.bfloat16):
    drawn = width * jax.random.normal(key, shape, jnp.float32)
    if cuts:
        drawn = drawn * block_levels(key, shape, cuts, -0.22, 0.18)
    return jnp.clip(drawn, -most, most).astype(dtype)


def setup_inputs(seed: int = 0) -> dict:
    arg_keys = jax.random.split(jax.random.key(seed), 10)
    return {
        "spectrum": jnp.clip(jnp.exp(math.log(2.0) - 2.9957323 * jax.random.uniform(arg_keys[0], (COMPS, LAT, LON), jnp.float32) ** block_levels(arg_keys[0], (COMPS, LAT, LON), ((0, 8), (2, 4)), -0.2, 0.2)), 0.1, 2.0),
        "land_mask": touch_ends((jax.random.randint(arg_keys[1], (LAT, LON), 0, 5) < 4).astype(jnp.int32), jax.random.fold_in(arg_keys[1], 1), 0, 1),
        "wind_field": noise(arg_keys[2], (2, LAT, LON), 0.5, 3.0, ((1, 8), (2, 4)), jnp.float32),
        "assignment": jax.random.permutation(arg_keys[3], COMPS).astype(jnp.int32),
        "courant": jnp.clip(jnp.exp(jax.random.uniform(arg_keys[4], (FREQ,), jnp.float32, math.log(0.3), math.log(0.65))), 0.3, 0.65),
        "growth": jnp.clip(jnp.exp(jax.random.uniform(arg_keys[5], (FREQ,), jnp.float32, math.log(0.1), math.log(0.5))), 0.1, 0.5),
        "whitecap": jnp.clip(jnp.exp(jax.random.uniform(arg_keys[6], (FREQ,), jnp.float32, math.log(0.2), math.log(1.0))), 0.2, 1.0),
        "weights": jnp.clip(jnp.exp(jax.random.uniform(arg_keys[7], (FREQ,), jnp.float32, math.log(0.5), math.log(5.0))), 0.5, 5.0),
        "spread": noise(arg_keys[8], (FREQ, DIRS, DIRS), DIRS ** -0.5, 1.0, (), jnp.float32),
    }


def flow_terms(kinds, courant):
    direction = kinds % DIRS
    frequency = kinds // DIRS
    angles = (direction.astype(jnp.float32) + 0.5) * (2.0 * math.pi / DIRS)
    speeds = courant[frequency]
    latitude = (jnp.arange(LAT).astype(jnp.float32) + 0.5 - LAT / 2) * (math.pi / 2160.0)
    flow_x = speeds[:, None] * jnp.cos(angles)[:, None] / jnp.cos(latitude)[None, :]
    flow_y = speeds * jnp.sin(angles)
    return flow_x, flow_y


def advance(wave_field, flow_x, flow_y, sea_mask):
    east_rate = jnp.maximum(flow_x, 0.0)[:, None]
    west_rate = jnp.maximum(-flow_x, 0.0)[:, None]
    north_rate = jnp.maximum(flow_y, 0.0)
    south_rate = jnp.maximum(-flow_y, 0.0)
    keep_rate = 1.0 - jnp.abs(flow_x)[:, None] - jnp.abs(flow_y)
    for substep in range(SUBSTEPS):
        from_west = jnp.roll(wave_field, 1, axis=1)
        from_east = jnp.roll(wave_field, -1, axis=1)
        from_south = jnp.pad(wave_field[:-1], ((1, 0), (0, 0)))
        from_north = jnp.pad(wave_field[1:], ((0, 1), (0, 0)))
        wave_field = (keep_rate * wave_field + east_rate * from_west + west_rate * from_east
                      + north_rate * from_south + south_rate * from_north) * sea_mask
    return wave_field


def source_tables(assignment, growth, whitecap, weights, spread):
    direction = assignment % DIRS
    frequency = assignment // DIRS
    angles = (direction.astype(jnp.float32) + 0.5) * (2.0 * math.pi / DIRS)
    picked_rows = spread.reshape(FREQ * DIRS, DIRS)[assignment]
    same_freq = (frequency[:, None] == frequency[None, :]).astype(jnp.float32)
    coupling = picked_rows[:, direction] * same_freq
    return (jnp.cos(angles), jnp.sin(angles), growth[frequency], whitecap[frequency],
            weights[frequency], coupling)


def relax(energy, wind_block, sea_row, tables):
    cosine, sine, growth_rows, whitecap_rows, weight_rows, coupling = tables
    loading = jnp.sum(weight_rows[:, None] * energy, axis=0) / COMPS
    drive = cosine[:, None] * wind_block[0][None, :] + sine[:, None] * wind_block[1][None, :]
    exponent = growth_rows[:, None] * jnp.maximum(drive, 0.0) - whitecap_rows[:, None] * (loading / (1.0 + loading))[None, :]
    mixed = jnp.dot(coupling, energy, precision=lax.Precision.HIGHEST)
    return (energy * jnp.exp(exponent) + 0.5 * mixed) * sea_row[None, :]


def reference(spectrum, land_mask, wind_field, assignment, courant, growth, whitecap, weights, spread):
    sea_mask = land_mask.astype(jnp.float32)
    flow_x, flow_y = flow_terms(assignment, courant)
    propagated = lax.map(lambda operand: advance(operand[0], operand[1], operand[2], sea_mask),
                         (spectrum, flow_x, flow_y))
    tables = source_tables(assignment, growth, whitecap, weights, spread)
    rows_first = lax.map(lambda operand: relax(operand[0], operand[1], operand[2], tables),
                         (jnp.moveaxis(propagated, 1, 0), jnp.moveaxis(wind_field, 1, 0), sea_mask))
    return jnp.moveaxis(rows_first, 0, 1)
```

```python
import math

import jax
import jax.numpy as jnp
from jax import lax
from jax.experimental import pallas as pl
from jax.experimental.pallas import tpu as pltpu
from jax.sharding import PartitionSpec as P


DIRS = 36
FREQ = 32
SUBSTEPS = 6
EDGE = 8
ROWS = 8
UNITS = 24
CHUNKS = (6, 6, 12)
STRIP_BLOCKS = 8
BAND = 4


def edge_strips(place, spectrum, turned_sea, base, made, block):
    _, lat, lon = spectrum.shape

    def kernel(place_ref, wave_ref, sea_ref, near_ref, far_ref, turned):
        step = pl.program_id(0)
        even = place_ref[1] == 0
        near = pl.multiple_of(jnp.where(even, lon - EDGE, 0), EDGE)
        far = pl.multiple_of(jnp.where(even, 0, lon - EDGE), EDGE)
        for b in range(block):
            turned[b] = wave_ref[b].T
            near_ref[step * block + b] = turned[b, pl.ds(near, EDGE)]
            far_ref[step * block + b] = turned[b, pl.ds(far, EDGE)]

        @pl.when(step == 0)
        def _():
            near_ref[made] = sea_ref[pl.ds(near, EDGE)]
            far_ref[made] = sea_ref[pl.ds(far, EDGE)]

    strip = pl.BlockSpec((made + 1, EDGE, lat), lambda i, *_: (0, 0, 0))
    shape = jax.ShapeDtypeStruct((made + 1, EDGE, lat), jnp.float32)
    first = base // block
    return pl.pallas_call(
        kernel,
        grid_spec=pltpu.PrefetchScalarGridSpec(
            num_scalar_prefetch=1,
            grid=(made // block,),
            in_specs=[
                pl.BlockSpec((block, lat, lon), lambda i, *_: (first + i, 0, 0)),
                pl.BlockSpec((lon, lat), lambda i, *_: (0, 0)),
            ],
            out_specs=[strip, strip],
            scratch_shapes=[pltpu.VMEM((block, lon, lat), jnp.float32)],
        ),
        out_shape=[shape, shape],
        cost_estimate=pl.CostEstimate(
            flops=0, bytes_accessed=8 * made * lat * lon, transcendentals=0
        ),
        name="edge_strips",
    )(place, spectrum, turned_sea)


def advance(tables, spectrum, strips, turned_sea, inverse, base, made, block, count, pieces):
    comps_dev, lat, lon = spectrum.shape
    rows_dev = sum(pieces)
    span = lon + EDGE
    tall = lon + 4 * EDGE
    lanes = 2 if block % 2 == 0 else 3 if block % 3 == 0 else 1
    north_row, south_row = 2 * EDGE + lon, EDGE

    def kernel(
        place_ref, kinds_ref, courant_ref, cos_ref, sin_ref,
        wave_ref, near_ref, far_ref, near_sea_ref, far_sea_ref, sea_ref, inverse_ref,
        *rest,
    ):
        outs, rest = rest[: len(pieces) * count], rest[len(pieces) * count :]
        sea, slope, side = rest[:3]
        sets = [rest[3 + 6 * q : 9 + 6 * q] for q in range(lanes)]
        step = pl.program_id(0)
        me = place_ref[0]
        even = place_ref[1] == 0
        near_row = pl.multiple_of(jnp.where(even, north_row, south_row), EDGE)
        far_row = pl.multiple_of(jnp.where(even, south_row, north_row), EDGE)

        @pl.when(step == 0)
        def _():
            for ping, pong, *_ in sets:
                ping[...] = jnp.zeros_like(ping)
                pong[...] = jnp.zeros_like(pong)
            sea[...] = jnp.zeros_like(sea)
            sea[2 * EDGE : 2 * EDGE + lon] = sea_ref[...]
            sea[pl.ds(near_row, EDGE)] = near_sea_ref[0]
            sea[pl.ds(far_row, EDGE)] = far_sea_ref[0]
            whole = sea[...]
            slope[...] = whole * inverse_ref[...]
            lane = lax.broadcasted_iota(jnp.int32, whole.shape, 1)
            side[0] = jnp.where(lane == 0, 0.0, whole)
            side[1] = jnp.where(lane == lat - 1, 0.0, whole)

        def some(i, carry):
            windows, upwinds, turns, heres = [], [], [], []
            for q, (ping, pong, keep, cross, along, result) in enumerate(sets):
                b = i * lanes + q
                kind = kinds_ref[me * comps_dev + base + step * block + b]
                speed = courant_ref[lax.div(kind, DIRS)]
                flow_x = speed * cos_ref[lax.rem(kind, DIRS)]
                flow_y = speed * sin_ref[lax.rem(kind, DIRS)]
                eastward = flow_x > 0.0
                northward = flow_y > 0.0
                first = pl.multiple_of(jnp.where(eastward, EDGE, 2 * EDGE), EDGE)
                windows.append(pl.ds(first, span))
                upwinds.append(pl.ds(jnp.where(eastward, EDGE - 1, 2 * EDGE + 1), span))
                turns.append(jnp.where(northward, 1, lat - 1))
                rate_x, rate_y = jnp.abs(flow_x), jnp.abs(flow_y)
                ratio = rate_x * slope[windows[q]]
                cross[...] = ratio
                along[...] = rate_y * side[jnp.where(northward, 0, 1), windows[q]]
                keep[...] = (1.0 - rate_y) * sea[windows[q]] - ratio
                ping[2 * EDGE : 2 * EDGE + lon] = wave_ref[b].T
                ping[pl.ds(near_row, EDGE)] = near_ref[b]
                ping[pl.ds(far_row, EDGE)] = far_ref[b]
            for q in range(lanes):
                heres.append(sets[q][0][windows[q]])
            for substep in range(SUBSTEPS):
                for q, (ping, pong, keep, cross, along, result) in enumerate(sets):
                    now, then = (ping, pong) if substep % 2 == 0 else (pong, ping)
                    heres[q] = (
                        keep[...] * heres[q]
                        + cross[...] * now[upwinds[q]]
                        + along[...] * pltpu.roll(heres[q], turns[q], 1)
                    )
                    then[windows[q]] = heres[q]
            for q, (ping, pong, keep, cross, along, result) in enumerate(sets):
                b = i * lanes + q
                last = ping if SUBSTEPS % 2 == 0 else pong
                result[...] = last[2 * EDGE : 2 * EDGE + lon].T
                offset = 0
                for p, rows in enumerate(pieces):
                    for k in range(count):
                        row = pl.multiple_of((me ^ k) * rows_dev + offset, ROWS)
                        outs[p * count + k][b] = result[pl.ds(row, rows)]
                    offset += rows
            return carry

        lax.fori_loop(0, block // lanes, some, 0)

    strip = pl.BlockSpec((block, EDGE, lat), lambda i, *_: (i, 0, 0))
    strip_of_sea = pl.BlockSpec((1, EDGE, lat), lambda i, *_: (made, 0, 0))
    fixed = lambda shape: pl.BlockSpec(shape, lambda i, *_: (0,) * len(shape))
    first_block = base // block
    f32 = lambda *shape: pltpu.VMEM(shape, jnp.float32)
    return pl.pallas_call(
        kernel,
        grid_spec=pltpu.PrefetchScalarGridSpec(
            num_scalar_prefetch=5,
            grid=(made // block,),
            in_specs=[
                pl.BlockSpec((block, lat, lon), lambda i, *_: (first_block + i, 0, 0)),
                strip,
                strip,
                strip_of_sea,
                strip_of_sea,
                fixed((lon, lat)),
                fixed((1, lat)),
            ],
            out_specs=[
                pl.BlockSpec((block, rows, lon), lambda i, *_: (i, 0, 0))
                for rows in pieces
                for _ in range(count)
            ],
            scratch_shapes=[f32(tall, lat), f32(tall, lat), f32(2, tall, lat)]
            + [
                f32(tall, lat), f32(tall, lat),
                f32(span, lat), f32(span, lat), f32(span, lat),
                f32(lat, lon),
            ] * lanes,
        ),
        out_shape=[
            jax.ShapeDtypeStruct((made, rows, lon), jnp.float32)
            for rows in pieces
            for _ in range(count)
        ],
        cost_estimate=pl.CostEstimate(
            flops=0, bytes_accessed=12 * made * lat * lon * 4, transcendentals=0
        ),
        name="advance",
    )(*tables, spectrum, *strips, *strips, turned_sea, inverse)


def couple(place, assignment, arrived, sea_rows, winds, per_kind, blocks, count, comps_dev, part):
    comps = assignment.shape[0]
    lon = sea_rows.shape[1]
    bands, band, _ = blocks[0].shape
    flat = [a for group, _ in arrived for a in group]
    sizes = [group[0].shape[0] for group, _ in arrived]
    unroll = 8 if all(size % 8 == 0 for size in sizes) else 6

    def kernel(place_ref, kinds_ref, *rest):
        ins, rest = rest[: len(flat)], rest[len(flat) :]
        sea_ref, wind_ref, weight_ref, east_ref, north_ref, decay_ref, high_ref, low_ref = rest[:8]
        outs, (sorted_ref,) = rest[8:-1], rest[-1:]
        me = place_ref[0]
        for k in range(count):
            for g in range(len(arrived)):
                first = (me ^ k) * comps_dev + sum(sizes[:g])
                source = ins[g * count + k]

                def put(i, carry, source=source, first=first):
                    rows = [i * unroll + u for u in range(unroll)]
                    kinds = [kinds_ref[first + c] for c in rows]
                    values = [source[c] for c in rows]
                    for kind, value in zip(kinds, values):
                        sorted_ref[pl.ds(kind, ROWS, stride=comps), :] = value
                    return carry

                lax.fori_loop(0, sizes[g] // unroll, put, 0)

        def pair(p, carry):
            starts = [pl.multiple_of((2 * p + q) * comps, 8) for q in range(2)]
            loads, us, vs, seas = [], [], [], []
            for q in range(2):
                j = 2 * p + q
                total = jnp.sum(
                    weight_ref[...] * sorted_ref[pl.ds(starts[q], comps), :], axis=0, keepdims=True
                )
                loading = total / comps
                loads.append(loading / (1.0 + loading))
                us.append(wind_ref[0, pl.ds(j, 1), :])
                vs.append(wind_ref[1, pl.ds(j, 1), :])
                seas.append(sea_ref[pl.ds(j, 1), :])
            for n in range(bands):
                kinds = slice(n * band, (n + 1) * band)
                spots = [pl.ds(pl.multiple_of(starts[q] + n * band, 8), band) for q in range(2)]
                energy = [sorted_ref[spots[q], :] for q in range(2)]
                both = jnp.concatenate(energy, axis=1)
                high = both.astype(jnp.bfloat16)
                low = (both - high.astype(jnp.float32)).astype(jnp.bfloat16)
                dot = lambda a, b: jnp.dot(a, b, preferred_element_type=jnp.float32)
                mixed = dot(high_ref[n], high) + (dot(high_ref[n], low) + dot(low_ref[n], high))
                for q in range(2):
                    drive = east_ref[kinds, :] * us[q] + north_ref[kinds, :] * vs[q]
                    exponent = jnp.maximum(drive, 0.0) - decay_ref[kinds, :] * loads[q]
                    sorted_ref[spots[q], :] = seas[q] * (
                        energy[q] * jnp.exp(exponent) + mixed[:, q * lon : (q + 1) * lon]
                    )
            return carry

        lax.fori_loop(0, ROWS // 2, pair, 0)
        step = 8 if comps_dev % 8 == 0 else 6
        for k in range(count):

            def take(i, carry, k=k):
                rows = [i * step + u for u in range(step)]
                kinds = [kinds_ref[(me ^ k) * comps_dev + c] for c in rows]
                values = [sorted_ref[pl.ds(kind, ROWS, stride=comps), :] for kind in kinds]
                for c, value in zip(rows, values):
                    outs[k][c] = value
                return carry

            lax.fori_loop(0, comps_dev // step, take, 0)

    vmem = pl.BlockSpec(memory_space=pltpu.VMEM)
    pieces = [
        pl.BlockSpec((a.shape[0], ROWS, lon), lambda *_, at=at: (0, at, 0))
        for group, at in arrived
        for a in group
    ]
    rows = pl.BlockSpec((ROWS, lon), lambda *_: (part, 0))
    wind_rows = pl.BlockSpec((2, ROWS, lon), lambda *_: (0, part, 0))
    return pl.pallas_call(
        kernel,
        grid_spec=pltpu.PrefetchScalarGridSpec(
            num_scalar_prefetch=2,
            grid=(1,),
            in_specs=pieces + [rows, wind_rows] + [vmem] * 6,
            out_specs=[vmem] * count,
            scratch_shapes=[pltpu.VMEM((ROWS * comps, lon), jnp.float32)],
        ),
        out_shape=[jax.ShapeDtypeStruct((comps_dev, ROWS, lon), jnp.float32)] * count,
        cost_estimate=pl.CostEstimate(
            flops=0, bytes_accessed=8 * comps * ROWS * lon * 4, transcendentals=0
        ),
        name="couple",
    )(place, assignment, *flat, sea_rows, winds, *per_kind, *blocks)


def settle(place, returned, ks, part, rows_dev, lat, partial):
    comps_dev, _, lon = returned[0].shape
    amount = len(ks)

    def kernel(place_ref, *rest):
        ins, out_ref, (held, in_sem, out_sem) = rest[:amount], rest[-4], rest[-3:]
        me = place_ref[0]
        into = [
            pltpu.make_async_copy(ins[n], held.at[n], in_sem.at[n]) for n in range(amount)
        ]
        for copy in into:
            copy.start()
        out = []
        for n, k in enumerate(ks):
            row = pl.multiple_of((me ^ k) * rows_dev + part * ROWS, ROWS)
            into[n].wait()
            out.append(
                pltpu.make_async_copy(
                    held.at[n], out_ref.at[:, pl.ds(row, ROWS), :], out_sem.at[n]
                )
            )
            out[n].start()
        for copy in out:
            copy.wait()

    anywhere = pl.BlockSpec(memory_space=pl.ANY)
    extra = [] if partial is None else [partial]
    return pl.pallas_call(
        kernel,
        grid_spec=pltpu.PrefetchScalarGridSpec(
            num_scalar_prefetch=1,
            grid=(),
            in_specs=[anywhere] * (amount + len(extra)),
            out_specs=anywhere,
            scratch_shapes=[
                pltpu.VMEM((amount, comps_dev, ROWS, lon), jnp.float32),
                pltpu.SemaphoreType.DMA((amount,)),
                pltpu.SemaphoreType.DMA((amount,)),
            ],
        ),
        out_shape=jax.ShapeDtypeStruct((comps_dev, lat, lon), jnp.float32),
        input_output_aliases={1 + amount: 0} if extra else {},
        cost_estimate=pl.CostEstimate(
            flops=0, bytes_accessed=2 * amount * comps_dev * ROWS * lon * 4, transcendentals=0
        ),
        name="settle",
    )(place, *[returned[k] for k in ks], *extra)


def order_of(count):
    return sorted(range(1, count), key=lambda k: (k == 1, k & 1, k))


def swap(pieces, count):
    made = [pieces[0]] + [None] * (count - 1)
    for k in order_of(count):
        made[k] = lax.ppermute(pieces[k], "group", [(i, i ^ k) for i in range(count)])
    return made


def exchange(near, far):
    count = lax.axis_size("sector")
    pairs = [(i, i ^ 1) for i in range(count)]
    near = lax.ppermute(near, "sector", pairs)
    pairs = [(i, (i + 1) % count if i % 2 else (i - 1) % count) for i in range(count)]
    far = lax.ppermute(far, "sector", pairs)
    return near, far


def local(spectrum, land_mask, wind_field, assignment, courant, growth, whitecap, weights, spread):
    member = lax.axis_index("group").astype(jnp.int32)
    count = lax.axis_size("group")
    comps_dev, lat, lon = spectrum.shape
    comps = assignment.shape[0]
    rows_dev = wind_field.shape[1]
    parts = rows_dev // ROWS
    unit = comps_dev // UNITS
    parity = lax.axis_index("sector").astype(jnp.int32) % 2
    place = jnp.stack((member, parity))

    angles = (jnp.arange(DIRS).astype(jnp.float32) + 0.5) * (2.0 * math.pi / DIRS)
    cosine, sine = jnp.cos(angles), jnp.sin(angles)
    latitude = (jnp.arange(lat).astype(jnp.float32) + 0.5 - lat / 2) * (math.pi / 2160.0)
    inverse = (1.0 / jnp.cos(latitude))[None, :]
    sea_mask = land_mask.astype(jnp.float32)
    turned = sea_mask.T
    tables = (place, assignment, courant, cosine, sine)

    arrived = [[] for _ in range(parts)]
    base = 0
    for c, units in enumerate(CHUNKS):
        made = units * unit
        near, far = edge_strips(
            place, spectrum, turned, base, made, comps_dev // STRIP_BLOCKS
        )
        strips = exchange(near, far)
        pieces = [ROWS] * parts if c == len(CHUNKS) - 1 else [rows_dev]
        sent = advance(tables, spectrum, strips, turned, inverse, base, made, unit, count, pieces)
        for p in range(len(pieces)):
            group = swap(sent[p * count : (p + 1) * count], count)
            for part in range(parts):
                if len(pieces) == 1:
                    arrived[part].append((group, part))
                elif p == part:
                    arrived[part].append((group, 0))
        base += made

    def spread_out(values):
        return jnp.broadcast_to(values[:, None], (comps, lon))

    fast = jnp.repeat(growth, DIRS)
    per_kind = (
        spread_out(jnp.repeat(weights, DIRS)),
        spread_out(fast * jnp.tile(cosine, FREQ)),
        spread_out(fast * jnp.tile(sine, FREQ)),
        spread_out(jnp.repeat(whitecap, DIRS)),
    )
    halves = (0.5 * spread).reshape(FREQ // BAND, BAND, DIRS, 1, DIRS)
    same = jnp.eye(BAND, dtype=jnp.float32)[None, :, None, :, None]
    whole = (halves * same).reshape(FREQ // BAND, BAND * DIRS, BAND * DIRS)
    high = lax.reduce_precision(whole, 8, 7)
    blocks = (high.astype(jnp.bfloat16), (whole - high).astype(jnp.bfloat16))
    sea_rows = lax.dynamic_slice_in_dim(sea_mask, member * rows_dev, rows_dev, 0)

    returned = []
    for part in range(parts):
        made = couple(
            place, assignment, arrived[part], sea_rows, wind_field, per_kind, blocks,
            count, comps_dev, part,
        )
        returned.append(swap(made, count))
    order = [0] + order_of(count)
    out = None
    for part in range(parts):
        cut = count if part < parts - 1 else (3 * count) // 4
        for ks in (order[:cut], order[cut:]):
            if ks:
                out = settle(place, returned[part], ks, part, rows_dev, lat, out)
    return out


def solution(mesh):
    in_specs = (
        P("group", None, "sector"),
        P(None, "sector"),
        P(None, "group", "sector"),
        P(),
        P(),
        P(),
        P(),
        P(),
        P(),
    )
    out_specs = P("group", None, "sector")
    return jax.shard_map(local, mesh=mesh, in_specs=in_specs, out_specs=out_specs, check_vma=False)
```

```python
import math

import jax
import jax.numpy as jnp
import numpy as np
from jax import lax
from jax.experimental import pallas as pl
from jax.experimental.pallas import tpu as pltpu
from jax.sharding import PartitionSpec as P


DIRS = 36
FREQ = 32
SUBSTEPS = 6
EDGE = 8
ROWS = 8
UNITS = 24
CHUNKS = (6, 8, 10)
STRIP_BLOCKS = 12
STREAMS = 3
BAND = 4
PAD = 8
LANES = 3


def edge_strips(spectrum, land_mask, base, made, block):
    _, lat, lon = spectrum.shape
    part = block // STREAMS

    def kernel(*rest):
        waves, (land_ref, near_ref, far_ref, turned) = rest[:STREAMS], rest[STREAMS:]
        step = pl.program_id(0)
        even = lax.rem(lax.axis_index("sector"), 2) == 0
        near = pl.multiple_of(jnp.where(even, lon - EDGE, 0), EDGE)
        far = pl.multiple_of(jnp.where(even, 0, lon - EDGE), EDGE)
        for b in range(block):
            turned[b] = waves[b // part][b % part].T
            near_ref[step * block + b] = turned[b, pl.ds(near, EDGE)]
            far_ref[step * block + b] = turned[b, pl.ds(far, EDGE)]

        @pl.when(step == 0)
        def _():
            turned[0] = land_ref[...].astype(jnp.float32).T
            near_ref[made] = turned[0, pl.ds(near, EDGE)]
            far_ref[made] = turned[0, pl.ds(far, EDGE)]

    strip = pl.BlockSpec((made + 1, EDGE, lat), lambda i, *_: (0, 0, 0))
    shape = jax.ShapeDtypeStruct((made + 1, EDGE, lat), jnp.float32)
    first = base // part
    streams = [
        pl.BlockSpec((part, lat, lon), lambda i, *_, n=n: (first + i * STREAMS + n, 0, 0))
        for n in range(STREAMS)
    ]
    return pl.pallas_call(
        kernel,
        grid=(made // block,),
        in_specs=streams + [pl.BlockSpec((lat, lon), lambda i: (0, 0))],
        out_specs=[strip, strip],
        scratch_shapes=[pltpu.VMEM((block, lon, lat), jnp.float32)],
        out_shape=[shape, shape],
        cost_estimate=pl.CostEstimate(
            flops=0, bytes_accessed=8 * made * lat * lon, transcendentals=0
        ),
        name="edge_strips",
    )(*[spectrum] * STREAMS, land_mask)


def advance(tables, spectrum, strips, land_mask, inverse, base, made, block, count, pieces):
    comps_dev, lat, lon = spectrum.shape
    rows_dev = sum(pieces)
    span = lon + EDGE
    lanes = LANES if block % LANES == 0 else 3 if block % 3 == 0 else 1

    def kernel(
        kinds_ref, courant_ref, cos_ref, sin_ref,
        wave_ref, near_ref, far_ref, near_sea_ref, far_sea_ref, land_ref, inverse_ref,
        *rest,
    ):
        outs, rest = rest[: len(pieces) * count], rest[len(pieces) * count :]
        sea, slope, side = rest[:3]
        sets = [rest[3 + 6 * q : 9 + 6 * q] for q in range(lanes)]
        step = pl.program_id(0)
        me = lax.axis_index("group")
        even = lax.rem(lax.axis_index("sector"), 2) == 0

        @pl.when(step == 0)
        def _():
            for ping, pong, *_ in sets:
                ping[...] = jnp.zeros_like(ping)
                pong[...] = jnp.zeros_like(pong)
            own = land_ref[...].astype(jnp.float32).T
            sea[0, EDGE:] = own
            sea[1, :lon] = own
            sea[0, :EDGE] = jnp.where(even, far_sea_ref[0], near_sea_ref[0])
            sea[1, lon:] = jnp.where(even, near_sea_ref[0], far_sea_ref[0])
            lane = lax.broadcasted_iota(jnp.int32, (span, lat), 1)
            for way in range(2):
                slope[way] = sea[way] * inverse_ref[...]
                side[way] = jnp.where(lane == 0, 0.0, sea[way])
                side[2 + way] = jnp.where(lane == lat - 1, 0.0, sea[way])

        def some(i, carry):
            easts, turns = [], []
            for q, (ping, pong, keep, cross, along, result) in enumerate(sets):
                b = i * lanes + q
                kind = kinds_ref[me * comps_dev + base + step * block + b]
                speed = courant_ref[lax.div(kind, DIRS)]
                flow_x = speed * cos_ref[lax.rem(kind, DIRS)]
                flow_y = speed * sin_ref[lax.rem(kind, DIRS)]
                eastward = flow_x > 0.0
                northward = flow_y > 0.0
                way = jnp.where(eastward, 0, 1)
                easts.append(jnp.full((EDGE, lat), way) == 0)
                turns.append(jnp.where(northward, 1, lat - 1))
                rate_x, rate_y = jnp.abs(flow_x), jnp.abs(flow_y)
                ratio = rate_x * slope[way]
                cross[...] = ratio
                along[...] = rate_y * side[jnp.where(northward, way, 2 + way)]
                keep[...] = (1.0 - rate_y) * sea[way] - ratio
                own = pl.multiple_of(jnp.where(eastward, 2 * EDGE, EDGE), EDGE)
                upwind = pl.multiple_of(jnp.where(eastward, EDGE, EDGE + lon), EDGE)
                ping[pl.ds(own, lon)] = wave_ref[b].T
                ping[pl.ds(upwind, EDGE)] = jnp.where(eastward == even, far_ref[b], near_ref[b])
            for substep in range(SUBSTEPS):
                for row in range(0, span, EDGE):
                    for q, (ping, pong, keep, cross, along, result) in enumerate(sets):
                        now, then = (ping, pong) if substep % 2 == 0 else (pong, ping)
                        spot = slice(row, row + EDGE)
                        here = now[row + EDGE : row + 2 * EDGE]
                        upwind = jnp.where(
                            easts[q],
                            now[row + EDGE - 1 : row + 2 * EDGE - 1],
                            now[row + EDGE + 1 : row + 2 * EDGE + 1],
                        )
                        then[row + EDGE : row + 2 * EDGE] = (
                            keep[spot] * here
                            + cross[spot] * upwind
                            + along[spot] * pltpu.roll(here, turns[q], 1)
                        )
            for q, (ping, pong, keep, cross, along, result) in enumerate(sets):
                b = i * lanes + q
                last = ping if SUBSTEPS % 2 == 0 else pong
                kind = kinds_ref[me * comps_dev + base + step * block + b]
                eastward = cos_ref[lax.rem(kind, DIRS)] > 0.0
                own = pl.multiple_of(jnp.where(eastward, 2 * EDGE, EDGE), EDGE)
                result[...] = last[pl.ds(own, lon)].T
                offset = 0
                for p, rows in enumerate(pieces):
                    for k in range(count):
                        row = pl.multiple_of((me ^ k) * rows_dev + offset, ROWS)
                        outs[p * count + k][b] = result[pl.ds(row, rows)]
                    offset += rows
            return carry

        lax.fori_loop(0, block // lanes, some, 0)

    strip = pl.BlockSpec((block, EDGE, lat), lambda i, *_: (i, 0, 0))
    strip_of_sea = pl.BlockSpec((1, EDGE, lat), lambda i, *_: (made, 0, 0))
    fixed = lambda shape: pl.BlockSpec(shape, lambda i, *_: (0,) * len(shape))
    first_block = base // block
    f32 = lambda *shape: pltpu.VMEM(shape, jnp.float32)
    return pl.pallas_call(
        kernel,
        grid_spec=pltpu.PrefetchScalarGridSpec(
            num_scalar_prefetch=4,
            grid=(made // block,),
            in_specs=[
                pl.BlockSpec((block, lat, lon), lambda i, *_: (first_block + i, 0, 0)),
                strip,
                strip,
                strip_of_sea,
                strip_of_sea,
                fixed((lat, lon)),
                fixed((1, lat)),
            ],
            out_specs=[
                pl.BlockSpec((block, rows, lon), lambda i, *_: (i, 0, 0))
                for rows in pieces
                for _ in range(count)
            ],
            scratch_shapes=[f32(2, span, lat), f32(2, span, lat), f32(4, span, lat)]
            + [
                f32(span + 2 * EDGE, lat), f32(span + 2 * EDGE, lat),
                f32(span, lat), f32(span, lat), f32(span, lat),
                f32(lat, lon),
            ] * lanes,
        ),
        out_shape=[
            jax.ShapeDtypeStruct((made, rows, lon), jnp.float32)
            for rows in pieces
            for _ in range(count)
        ],
        cost_estimate=pl.CostEstimate(
            flops=0, bytes_accessed=12 * made * lat * lon * 4, transcendentals=0
        ),
        name="advance",
    )(*tables, spectrum, *strips, *strips, land_mask, inverse)


def couple(assignment, arrived, sea_rows, winds, per_kind, blocks, count, comps_dev, part):
    comps = assignment.shape[0]
    lon = sea_rows.shape[1]
    bands, band, _ = blocks[0].shape
    flat = [a for group, _ in arrived for a in group]
    sizes = [group[0].shape[0] for group, _ in arrived]
    pitch = comps + PAD
    unroll = 8 if all(size % 8 == 0 for size in sizes) else 6

    def kernel(kinds_ref, *rest):
        ins, rest = rest[: len(flat)], rest[len(flat) :]
        sea_ref, wind_ref, weight_ref, east_ref, north_ref, decay_ref, high_ref, low_ref = rest[:8]
        outs, (sorted_ref,) = rest[8:-1], rest[-1:]
        me = lax.axis_index("group")
        for k in range(count):
            for g in range(len(arrived)):
                first = (me ^ k) * comps_dev + sum(sizes[:g])
                source = ins[g * count + k]

                def put(i, carry, source=source, first=first):
                    rows = [i * unroll + u for u in range(unroll)]
                    kinds = [kinds_ref[first + c] for c in rows]
                    values = [source[c] for c in rows]
                    for kind, value in zip(kinds, values):
                        sorted_ref[pl.ds(kind, ROWS, stride=pitch), :] = value
                    return carry

                lax.fori_loop(0, sizes[g] // unroll, put, 0)

        def pair(p, carry):
            starts = [pl.multiple_of((2 * p + q) * pitch, 8) for q in range(2)]
            loads, us, vs, seas = [], [], [], []
            for q in range(2):
                j = 2 * p + q
                total = jnp.sum(
                    weight_ref[...] * sorted_ref[pl.ds(starts[q], comps), :], axis=0, keepdims=True
                )
                loading = total / comps
                loads.append(loading / (1.0 + loading))
                us.append(wind_ref[0, pl.ds(j, 1), :])
                vs.append(wind_ref[1, pl.ds(j, 1), :])
                seas.append(sea_ref[pl.ds(j, 1), :])
            for n in range(bands):
                kinds = slice(n * band, (n + 1) * band)
                spots = [pl.ds(pl.multiple_of(starts[q] + n * band, 8), band) for q in range(2)]
                energy = [sorted_ref[spots[q], :] for q in range(2)]
                both = jnp.concatenate(energy, axis=1)
                high = both.astype(jnp.bfloat16)
                low = (both - high.astype(jnp.float32)).astype(jnp.bfloat16)
                dot = lambda a, b: jnp.dot(a, b, preferred_element_type=jnp.float32)
                mixed = dot(high_ref[n], high) + (dot(high_ref[n], low) + dot(low_ref[n], high))
                for q in range(2):
                    drive = east_ref[kinds, :] * us[q] + north_ref[kinds, :] * vs[q]
                    exponent = jnp.maximum(drive, 0.0) - decay_ref[kinds, :] * loads[q]
                    sorted_ref[spots[q], :] = seas[q] * (
                        energy[q] * jnp.exp(exponent) + mixed[:, q * lon : (q + 1) * lon]
                    )
            return carry

        lax.fori_loop(0, ROWS // 2, pair, 0)
        step = 8 if comps_dev % 8 == 0 else 6
        for k in range(count):

            def take(i, carry, k=k):
                rows = [i * step + u for u in range(step)]
                kinds = [kinds_ref[(me ^ k) * comps_dev + c] for c in rows]
                values = [sorted_ref[pl.ds(kind, ROWS, stride=pitch), :] for kind in kinds]
                for c, value in zip(rows, values):
                    outs[k][c] = value
                return carry

            lax.fori_loop(0, comps_dev // step, take, 0)

    vmem = pl.BlockSpec(memory_space=pltpu.VMEM)
    pieces = [
        pl.BlockSpec((a.shape[0], ROWS, lon), lambda *_, at=at: (0, at, 0))
        for group, at in arrived
        for a in group
    ]
    rows = pl.BlockSpec((ROWS, lon), lambda *_: (part, 0))
    wind_rows = pl.BlockSpec((2, ROWS, lon), lambda *_: (0, part, 0))
    return pl.pallas_call(
        kernel,
        grid_spec=pltpu.PrefetchScalarGridSpec(
            num_scalar_prefetch=1,
            grid=(1,),
            in_specs=pieces + [rows, wind_rows] + [vmem] * 6,
            out_specs=[vmem] * count,
            scratch_shapes=[pltpu.VMEM((ROWS * pitch, lon), jnp.float32)],
        ),
        out_shape=[jax.ShapeDtypeStruct((comps_dev, ROWS, lon), jnp.float32)] * count,
        cost_estimate=pl.CostEstimate(
            flops=0, bytes_accessed=8 * comps * ROWS * lon * 4, transcendentals=0
        ),
        name="couple",
    )(assignment, *flat, sea_rows, winds, *per_kind, *blocks)


def settle(returned, ks, part, rows_dev, lat, partial):
    comps_dev, _, lon = returned[0].shape
    cuts = 4 if len(ks) <= 2 else 2
    cut = comps_dev // cuts
    jobs = [(n, k, c) for n, k in enumerate(ks) for c in range(cuts)]
    amount = len(jobs)

    def kernel(*rest):
        ins, out_ref, (held, in_sem, out_sem) = rest[: len(ks)], rest[-4], rest[-3:]
        me = lax.axis_index("group")
        into, out = [], []
        for job, (n, k, c) in enumerate(jobs):
            row = pl.multiple_of((me ^ k) * rows_dev + part * ROWS, ROWS)
            some = pl.ds(c * cut, cut)
            into.append(pltpu.make_async_copy(ins[n].at[some], held.at[job], in_sem.at[job]))
            target = out_ref.at[some, pl.ds(row, ROWS), :]
            out.append(pltpu.make_async_copy(held.at[job], target, out_sem.at[job]))
        for copy in into:
            copy.start()
        for job in range(amount):
            into[job].wait()
            out[job].start()
        for copy in out:
            copy.wait()

    anywhere = pl.BlockSpec(memory_space=pl.ANY)
    extra = [] if partial is None else [partial]
    return pl.pallas_call(
        kernel,
        in_specs=[anywhere] * (len(ks) + len(extra)),
        out_specs=anywhere,
        scratch_shapes=[
            pltpu.VMEM((amount, cut, ROWS, lon), jnp.float32),
            pltpu.SemaphoreType.DMA((amount,)),
            pltpu.SemaphoreType.DMA((amount,)),
        ],
        out_shape=jax.ShapeDtypeStruct((comps_dev, lat, lon), jnp.float32),
        input_output_aliases={len(ks): 0} if extra else {},
        cost_estimate=pl.CostEstimate(
            flops=0, bytes_accessed=2 * len(ks) * comps_dev * ROWS * lon * 4, transcendentals=0
        ),
        name="settle",
    )(*[returned[k] for k in ks], *extra)


def order_of(count):
    return [k for k in (*range(2, count, 2), *range(3, count, 2))] + [1]


def stages_of(count):
    order = order_of(count)
    return [[0, 1] + order[: count - 5], order[count - 5 : count - 3], order[count - 3 : count - 2]]


def swap(pieces, count):
    made = [pieces[0]] + [None] * (count - 1)
    for k in order_of(count):
        made[k] = lax.ppermute(pieces[k], "group", [(i, i ^ k) for i in range(count)])
    return made


def exchange(near, far):
    count = lax.axis_size("sector")
    pairs = [(i, i ^ 1) for i in range(count)]
    near = lax.ppermute(near, "sector", pairs)
    pairs = [(i, (i + 1) % count if i % 2 else (i - 1) % count) for i in range(count)]
    far = lax.ppermute(far, "sector", pairs)
    return near, far


def local(spectrum, land_mask, wind_field, assignment, courant, growth, whitecap, weights, spread):
    member = lax.axis_index("group").astype(jnp.int32)
    count = lax.axis_size("group")
    comps_dev, lat, lon = spectrum.shape
    comps = assignment.shape[0]
    rows_dev = wind_field.shape[1]
    parts = rows_dev // ROWS
    unit = comps_dev // UNITS

    angles = (np.arange(DIRS) + 0.5) * (2.0 * math.pi / DIRS)
    cosine = jnp.asarray(np.cos(angles), jnp.float32)
    sine = jnp.asarray(np.sin(angles), jnp.float32)
    latitude = (np.arange(lat) + 0.5 - lat / 2) * (math.pi / 2160.0)
    inverse = jnp.asarray(1.0 / np.cos(latitude), jnp.float32)[None, :]
    sea_mask = land_mask.astype(jnp.float32)
    tables = (assignment, courant, cosine, sine)

    arrived = [[] for _ in range(parts)]
    base = 0
    for c, units in enumerate(CHUNKS):
        made = units * unit
        near, far = edge_strips(
            spectrum, land_mask, base, made, comps_dev // STRIP_BLOCKS
        )
        strips = exchange(near, far)
        pieces = [ROWS] * parts if c == len(CHUNKS) - 1 else [rows_dev]
        sent = advance(
            tables, spectrum, strips, land_mask, inverse, base, made, unit, count, pieces
        )
        for p in range(len(pieces)):
            group = swap(sent[p * count : (p + 1) * count], count)
            for part in range(parts):
                if len(pieces) == 1:
                    arrived[part].append((group, part))
                elif p == part:
                    arrived[part].append((group, 0))
        base += made

    def spread_out(values):
        return jnp.broadcast_to(values[:, None], (comps, lon))

    fast = jnp.repeat(growth, DIRS)
    per_kind = (
        spread_out(jnp.repeat(weights, DIRS)),
        spread_out(fast * jnp.tile(cosine, FREQ)),
        spread_out(fast * jnp.tile(sine, FREQ)),
        spread_out(jnp.repeat(whitecap, DIRS)),
    )
    halves = (0.5 * spread).reshape(FREQ // BAND, BAND, DIRS, 1, DIRS)
    same = jnp.eye(BAND, dtype=jnp.float32)[None, :, None, :, None]
    whole = (halves * same).reshape(FREQ // BAND, BAND * DIRS, BAND * DIRS)
    high = lax.reduce_precision(whole, 8, 7)
    blocks = (high.astype(jnp.bfloat16), (whole - high).astype(jnp.bfloat16))
    sea_rows = lax.dynamic_slice_in_dim(sea_mask, member * rows_dev, rows_dev, 0)

    returned = []
    for part in range(parts):
        made = couple(
            assignment, arrived[part], sea_rows, wind_field, per_kind, blocks,
            count, comps_dev, part,
        )
        returned.append(swap(made, count))
    order = order_of(count)
    out = None
    for part in range(parts):
        stages = [[0] + order] if part < parts - 1 else stages_of(count)
        for ks in stages:
            out = settle(returned[part], ks, part, rows_dev, lat, out)
    return out


def solution(mesh):
    in_specs = (
        P("group", None, "sector"),
        P(None, "sector"),
        P(None, "group", "sector"),
        P(),
        P(),
        P(),
        P(),
        P(),
        P(),
    )
    out_specs = P("group", None, "sector")
    return jax.shard_map(local, mesh=mesh, in_specs=in_specs, out_specs=out_specs, check_vma=False)
```

```python
import math

import jax
import jax.numpy as jnp
import numpy as np
from jax import lax
from jax.experimental import pallas as pl
from jax.experimental.pallas import tpu as pltpu
from jax.sharding import PartitionSpec as P


DIRS = 36
SUBSTEPS = 6
EDGE = 8
ROWS = 8
UNITS = 24
CHUNKS = (7, 7, 10)
STRIP_BLOCKS = 10
STREAMS = 3
BAND = 4
PAD = 8
LANES = 3


def strip_blocks(base, made, most):
    for block in range(most, 0, -1):
        for streams in range(STREAMS, 0, -1):
            part = block // streams
            if made % block == 0 and block % streams == 0 and base % part == 0:
                return block, streams


def edge_strips(spectrum, land_mask, base, made, most):
    _, lat, lon = spectrum.shape
    block, copies = strip_blocks(base, made, most)
    part = block // copies

    def kernel(*rest):
        waves, (land_ref, near_ref, far_ref, turned) = rest[:copies], rest[copies:]
        step = pl.program_id(0)
        even = lax.rem(lax.axis_index("sector"), 2) == 0
        near = pl.multiple_of(jnp.where(even, lon - EDGE, 0), EDGE)
        far = pl.multiple_of(jnp.where(even, 0, lon - EDGE), EDGE)
        for b in range(block):
            turned[b] = waves[b // part][b % part].T
            near_ref[step * block + b] = turned[b, pl.ds(near, EDGE)]
            far_ref[step * block + b] = turned[b, pl.ds(far, EDGE)]

        @pl.when(step == 0)
        def _():
            turned[0] = land_ref[...].astype(jnp.float32).T
            near_ref[made] = turned[0, pl.ds(near, EDGE)]
            far_ref[made] = turned[0, pl.ds(far, EDGE)]

    strip = pl.BlockSpec((made + 1, EDGE, lat), lambda i, *_: (0, 0, 0))
    shape = jax.ShapeDtypeStruct((made + 1, EDGE, lat), jnp.float32)
    first = base // part
    streams = [
        pl.BlockSpec((part, lat, lon), lambda i, *_, n=n: (first + i * copies + n, 0, 0))
        for n in range(copies)
    ]
    return pl.pallas_call(
        kernel,
        grid=(made // block,),
        in_specs=streams + [pl.BlockSpec((lat, lon), lambda i: (0, 0))],
        out_specs=[strip, strip],
        scratch_shapes=[pltpu.VMEM((block, lon, lat), jnp.float32)],
        out_shape=[shape, shape],
        cost_estimate=pl.CostEstimate(
            flops=0, bytes_accessed=8 * made * lat * lon, transcendentals=0
        ),
        name="edge_strips",
    )(*[spectrum] * copies, land_mask)


def advance(tables, spectrum, strips, land_mask, inverse, base, made, block, count, pieces):
    comps_dev, lat, lon = spectrum.shape
    rows_dev = sum(pieces)
    span = lon + EDGE
    lanes = LANES if block % LANES == 0 else 3 if block % 3 == 0 else 1

    def kernel(
        kinds_ref, courant_ref, cos_ref, sin_ref,
        wave_ref, near_ref, far_ref, near_sea_ref, far_sea_ref, land_ref, inverse_ref,
        *rest,
    ):
        outs, rest = rest[: len(pieces) * count], rest[len(pieces) * count :]
        sea, slope, side = rest[:3]
        sets = [rest[3 + 6 * q : 9 + 6 * q] for q in range(lanes)]
        step = pl.program_id(0)
        me = lax.axis_index("group")
        even = lax.rem(lax.axis_index("sector"), 2) == 0

        @pl.when(step == 0)
        def _():
            for ping, pong, *_ in sets:
                ping[...] = jnp.zeros_like(ping)
                pong[...] = jnp.zeros_like(pong)
            own = land_ref[...].astype(jnp.float32).T
            sea[0, EDGE:] = own
            sea[1, :lon] = own
            sea[0, :EDGE] = jnp.where(even, far_sea_ref[0], near_sea_ref[0])
            sea[1, lon:] = jnp.where(even, near_sea_ref[0], far_sea_ref[0])
            lane = lax.broadcasted_iota(jnp.int32, (span, lat), 1)
            for way in range(2):
                slope[way] = sea[way] * inverse_ref[...]
                side[way] = jnp.where(lane == 0, 0.0, sea[way])
                side[2 + way] = jnp.where(lane == lat - 1, 0.0, sea[way])

        def some(i, carry):
            easts, turns = [], []
            for q, (ping, pong, keep, cross, along, result) in enumerate(sets):
                b = i * lanes + q
                kind = kinds_ref[me * comps_dev + base + step * block + b]
                speed = courant_ref[lax.div(kind, DIRS)]
                flow_x = speed * cos_ref[lax.rem(kind, DIRS)]
                flow_y = speed * sin_ref[lax.rem(kind, DIRS)]
                eastward = flow_x > 0.0
                northward = flow_y > 0.0
                way = jnp.where(eastward, 0, 1)
                easts.append(jnp.full((EDGE, lat), way) == 0)
                turns.append(jnp.where(northward, 1, lat - 1))
                rate_x, rate_y = jnp.abs(flow_x), jnp.abs(flow_y)
                ratio = rate_x * slope[way]
                cross[...] = ratio
                along[...] = rate_y * side[jnp.where(northward, way, 2 + way)]
                keep[...] = (1.0 - rate_y) * sea[way] - ratio
                own = pl.multiple_of(jnp.where(eastward, 2 * EDGE, EDGE), EDGE)
                upwind = pl.multiple_of(jnp.where(eastward, EDGE, EDGE + lon), EDGE)
                ping[pl.ds(own, lon)] = wave_ref[b].T
                ping[pl.ds(upwind, EDGE)] = jnp.where(eastward == even, far_ref[b], near_ref[b])
            for substep in range(SUBSTEPS):
                for row in range(0, span, EDGE):
                    for q, (ping, pong, keep, cross, along, result) in enumerate(sets):
                        now, then = (ping, pong) if substep % 2 == 0 else (pong, ping)
                        spot = slice(row, row + EDGE)
                        here = now[row + EDGE : row + 2 * EDGE]
                        upwind = jnp.where(
                            easts[q],
                            now[row + EDGE - 1 : row + 2 * EDGE - 1],
                            now[row + EDGE + 1 : row + 2 * EDGE + 1],
                        )
                        then[row + EDGE : row + 2 * EDGE] = (
                            keep[spot] * here
                            + cross[spot] * upwind
                            + along[spot] * pltpu.roll(here, turns[q], 1)
                        )
            for q, (ping, pong, keep, cross, along, result) in enumerate(sets):
                b = i * lanes + q
                last = ping if SUBSTEPS % 2 == 0 else pong
                kind = kinds_ref[me * comps_dev + base + step * block + b]
                eastward = cos_ref[lax.rem(kind, DIRS)] > 0.0
                own = pl.multiple_of(jnp.where(eastward, 2 * EDGE, EDGE), EDGE)
                result[...] = last[pl.ds(own, lon)].T
                offset = 0
                for p, rows in enumerate(pieces):
                    for k in range(count):
                        row = pl.multiple_of((me ^ k) * rows_dev + offset, ROWS)
                        outs[p * count + k][b] = result[pl.ds(row, rows)]
                    offset += rows
            return carry

        lax.fori_loop(0, block // lanes, some, 0)

    strip = pl.BlockSpec((block, EDGE, lat), lambda i, *_: (i, 0, 0))
    strip_of_sea = pl.BlockSpec((1, EDGE, lat), lambda i, *_: (made, 0, 0))
    fixed = lambda shape: pl.BlockSpec(shape, lambda i, *_: (0,) * len(shape))
    first_block = base // block
    f32 = lambda *shape: pltpu.VMEM(shape, jnp.float32)
    return pl.pallas_call(
        kernel,
        grid_spec=pltpu.PrefetchScalarGridSpec(
            num_scalar_prefetch=4,
            grid=(made // block,),
            in_specs=[
                pl.BlockSpec((block, lat, lon), lambda i, *_: (first_block + i, 0, 0)),
                strip,
                strip,
                strip_of_sea,
                strip_of_sea,
                fixed((lat, lon)),
                fixed((1, lat)),
            ],
            out_specs=[
                pl.BlockSpec((block, rows, lon), lambda i, *_: (i, 0, 0))
                for rows in pieces
                for _ in range(count)
            ],
            scratch_shapes=[f32(2, span, lat), f32(2, span, lat), f32(4, span, lat)]
            + [
                f32(span + 2 * EDGE, lat), f32(span + 2 * EDGE, lat),
                f32(span, lat), f32(span, lat), f32(span, lat),
                f32(lat, lon),
            ] * lanes,
        ),
        out_shape=[
            jax.ShapeDtypeStruct((made, rows, lon), jnp.float32)
            for rows in pieces
            for _ in range(count)
        ],
        cost_estimate=pl.CostEstimate(
            flops=0, bytes_accessed=12 * made * lat * lon * 4, transcendentals=0
        ),
        name="advance",
    )(*tables, spectrum, *strips, *strips, land_mask, inverse)


def coupling_tables(growth, whitecap, weights, spread, cosine, sine, after, lon):
    freqs, dirs, _ = spread.shape
    comps = freqs * dirs
    bands, band = freqs // BAND, BAND * dirs

    def kernel(growth_ref, decay_ref, weight_ref, spread_ref, cos_ref, sin_ref, _, *rest):
        weights_ref, east_ref, north_ref, decays_ref, high_ref, low_ref, whole = rest
        one = jnp.ones((dirs, lon), jnp.float32)
        for f in range(freqs):
            rows = slice(f * dirs, (f + 1) * dirs)
            weights_ref[rows] = weight_ref[f] * one
            east_ref[rows] = growth_ref[f] * cos_ref[...]
            north_ref[rows] = growth_ref[f] * sin_ref[...]
            decays_ref[rows] = decay_ref[f] * one
        whole[...] = jnp.zeros_like(whole)
        for n in range(bands):
            for q in range(BAND):
                spot = slice(q * dirs, (q + 1) * dirs)
                whole[spot, spot] = 0.5 * spread_ref[n * BAND + q]
            high = whole[...].astype(jnp.bfloat16)
            high_ref[n] = high
            low_ref[n] = (whole[...] - high.astype(jnp.float32)).astype(jnp.bfloat16)

    scalars = pl.BlockSpec(memory_space=pltpu.SMEM)
    vmem = pl.BlockSpec(memory_space=pltpu.VMEM)
    spread_out = lambda values: jnp.asarray(np.repeat(values[:, None], lon, axis=1))
    rates = jax.ShapeDtypeStruct((comps, lon), jnp.float32)
    part = jax.ShapeDtypeStruct((bands, band, band), jnp.bfloat16)
    made = pl.pallas_call(
        kernel,
        in_specs=[scalars] * 3 + [vmem] * 3 + [pl.BlockSpec(memory_space=pl.ANY)],
        out_specs=[vmem] * 6,
        out_shape=[rates] * 4 + [part] * 2,
        scratch_shapes=[pltpu.VMEM((band, band), jnp.float32)],
        cost_estimate=pl.CostEstimate(
            flops=0, bytes_accessed=20 * comps * lon, transcendentals=0
        ),
        name="coupling_tables",
    )(growth, whitecap, weights, spread, spread_out(cosine), spread_out(sine), after)
    return made[:4], made[4:]


def couple(assignment, arrived, land_mask, winds, per_kind, blocks, count, comps_dev, part):
    comps = assignment.shape[0]
    lon = land_mask.shape[1]
    rows_dev = winds.shape[1]
    bands, band, _ = blocks[0].shape
    flat = [a for group, _ in arrived for a in group]
    sizes = [group[0].shape[0] for group, _ in arrived]
    pitch = comps + PAD
    unroll = 8 if all(size % 8 == 0 for size in sizes) else 6

    def kernel(kinds_ref, *rest):
        ins, rest = rest[: len(flat)], rest[len(flat) :]
        land_ref, wind_ref, weight_ref, east_ref, north_ref, decay_ref, high_ref, low_ref = rest[:8]
        outs, (sorted_ref,) = rest[8:-1], rest[-1:]
        me = lax.axis_index("group")
        for k in range(count):
            for g in range(len(arrived)):
                first = (me ^ k) * comps_dev + sum(sizes[:g])
                source = ins[g * count + k]

                def put(i, carry, source=source, first=first):
                    rows = [i * unroll + u for u in range(unroll)]
                    kinds = [kinds_ref[first + c] for c in rows]
                    values = [source[c] for c in rows]
                    for kind, value in zip(kinds, values):
                        sorted_ref[pl.ds(kind, ROWS, stride=pitch), :] = value
                    return carry

                lax.fori_loop(0, sizes[g] // unroll, put, 0)

        def pair(p, carry):
            starts = [pl.multiple_of((2 * p + q) * pitch, 8) for q in range(2)]
            loads, us, vs, seas = [], [], [], []
            for q in range(2):
                j = 2 * p + q
                total = jnp.sum(
                    weight_ref[...] * sorted_ref[pl.ds(starts[q], comps), :], axis=0, keepdims=True
                )
                loading = total / comps
                loads.append(loading / (1.0 + loading))
                us.append(wind_ref[0, pl.ds(j, 1), :])
                vs.append(wind_ref[1, pl.ds(j, 1), :])
                sea_row = land_ref[pl.ds(me * rows_dev + part * ROWS + j, 1), :]
                seas.append(sea_row.astype(jnp.float32))
            for n in range(bands):
                kinds = slice(n * band, (n + 1) * band)
                spots = [pl.ds(pl.multiple_of(starts[q] + n * band, 8), band) for q in range(2)]
                energy = [sorted_ref[spots[q], :] for q in range(2)]
                both = jnp.concatenate(energy, axis=1)
                high = both.astype(jnp.bfloat16)
                low = (both - high.astype(jnp.float32)).astype(jnp.bfloat16)
                dot = lambda a, b: jnp.dot(a, b, preferred_element_type=jnp.float32)
                mixed = dot(high_ref[n], high) + (dot(high_ref[n], low) + dot(low_ref[n], high))
                for q in range(2):
                    drive = east_ref[kinds, :] * us[q] + north_ref[kinds, :] * vs[q]
                    exponent = jnp.maximum(drive, 0.0) - decay_ref[kinds, :] * loads[q]
                    sorted_ref[spots[q], :] = seas[q] * (
                        energy[q] * jnp.exp(exponent) + mixed[:, q * lon : (q + 1) * lon]
                    )
            return carry

        lax.fori_loop(0, ROWS // 2, pair, 0)
        step = 8 if comps_dev % 8 == 0 else 6
        for k in range(count):

            def take(i, carry, k=k):
                rows = [i * step + u for u in range(step)]
                kinds = [kinds_ref[(me ^ k) * comps_dev + c] for c in rows]
                values = [sorted_ref[pl.ds(kind, ROWS, stride=pitch), :] for kind in kinds]
                for c, value in zip(rows, values):
                    outs[k][c] = value
                return carry

            lax.fori_loop(0, comps_dev // step, take, 0)

    vmem = pl.BlockSpec(memory_space=pltpu.VMEM)
    pieces = [
        pl.BlockSpec((a.shape[0], ROWS, lon), lambda *_, at=at: (0, at, 0))
        for group, at in arrived
        for a in group
    ]
    wind_rows = pl.BlockSpec((2, ROWS, lon), lambda *_: (0, part, 0))
    return pl.pallas_call(
        kernel,
        grid_spec=pltpu.PrefetchScalarGridSpec(
            num_scalar_prefetch=1,
            grid=(1,),
            in_specs=pieces + [vmem, wind_rows] + [vmem] * 6,
            out_specs=[vmem] * count,
            scratch_shapes=[pltpu.VMEM((ROWS * pitch, lon), jnp.float32)],
        ),
        out_shape=[jax.ShapeDtypeStruct((comps_dev, ROWS, lon), jnp.float32)] * count,
        cost_estimate=pl.CostEstimate(
            flops=0, bytes_accessed=8 * comps * ROWS * lon * 4, transcendentals=0
        ),
        name="couple",
    )(assignment, *flat, land_mask, winds, *per_kind, *blocks)


def settle(returned, ks, part, rows_dev, lat, partial):
    comps_dev, _, lon = returned[0].shape
    cuts = 4 if len(ks) <= 2 else 2
    cut = comps_dev // cuts
    jobs = [(n, k, c) for n, k in enumerate(ks) for c in range(cuts)]
    amount = len(jobs)

    def kernel(*rest):
        ins, out_ref, (held, in_sem, out_sem) = rest[: len(ks)], rest[-4], rest[-3:]
        me = lax.axis_index("group")
        into, out = [], []
        for job, (n, k, c) in enumerate(jobs):
            row = pl.multiple_of((me ^ k) * rows_dev + part * ROWS, ROWS)
            some = pl.ds(c * cut, cut)
            into.append(pltpu.make_async_copy(ins[n].at[some], held.at[job], in_sem.at[job]))
            target = out_ref.at[some, pl.ds(row, ROWS), :]
            out.append(pltpu.make_async_copy(held.at[job], target, out_sem.at[job]))
        for copy in into:
            copy.start()
        for job in range(amount):
            into[job].wait()
            out[job].start()
        for copy in out:
            copy.wait()

    anywhere = pl.BlockSpec(memory_space=pl.ANY)
    extra = [] if partial is None else [partial]
    return pl.pallas_call(
        kernel,
        in_specs=[anywhere] * (len(ks) + len(extra)),
        out_specs=anywhere,
        scratch_shapes=[
            pltpu.VMEM((amount, cut, ROWS, lon), jnp.float32),
            pltpu.SemaphoreType.DMA((amount,)),
            pltpu.SemaphoreType.DMA((amount,)),
        ],
        out_shape=jax.ShapeDtypeStruct((comps_dev, lat, lon), jnp.float32),
        input_output_aliases={len(ks): 0} if extra else {},
        cost_estimate=pl.CostEstimate(
            flops=0, bytes_accessed=2 * len(ks) * comps_dev * ROWS * lon * 4, transcendentals=0
        ),
        name="settle",
    )(*[returned[k] for k in ks], *extra)


def order_of(count):
    return [k for k in (*range(2, count, 2), *range(3, count, 2))] + [1]


def stages_of(count):
    order = order_of(count)
    return [[0, 1] + order[: count - 5], order[count - 5 : count - 4], order[count - 4 : count - 2]]


def swap(pieces, count):
    made = [pieces[0]] + [None] * (count - 1)
    for k in order_of(count):
        made[k] = lax.ppermute(pieces[k], "group", [(i, i ^ k) for i in range(count)])
    return made


def exchange(near, far):
    count = lax.axis_size("sector")
    pairs = [(i, i ^ 1) for i in range(count)]
    near = lax.ppermute(near, "sector", pairs)
    pairs = [(i, (i + 1) % count if i % 2 else (i - 1) % count) for i in range(count)]
    far = lax.ppermute(far, "sector", pairs)
    return near, far


def local(spectrum, land_mask, wind_field, assignment, courant, growth, whitecap, weights, spread):
    count = lax.axis_size("group")
    comps_dev, lat, lon = spectrum.shape
    rows_dev = wind_field.shape[1]
    parts = rows_dev // ROWS
    unit = comps_dev // UNITS

    angles = (np.arange(DIRS) + 0.5) * (2.0 * math.pi / DIRS)
    cosine, sine = np.float32(np.cos(angles)), np.float32(np.sin(angles))
    latitude = (np.arange(lat) + 0.5 - lat / 2) * (math.pi / 2160.0)
    inverse = jnp.asarray(1.0 / np.cos(latitude), jnp.float32)[None, :]
    tables = (assignment, courant, jnp.asarray(cosine), jnp.asarray(sine))

    arrived = [[] for _ in range(parts)]
    base = 0
    for c, units in enumerate(CHUNKS):
        made = units * unit
        near, far = edge_strips(
            spectrum, land_mask, base, made, comps_dev // STRIP_BLOCKS
        )
        strips = exchange(near, far)
        pieces = [ROWS] * parts if c == len(CHUNKS) - 1 else [rows_dev]
        sent = advance(
            tables, spectrum, strips, land_mask, inverse, base, made, unit, count, pieces
        )
        for p in range(len(pieces)):
            group = swap(sent[p * count : (p + 1) * count], count)
            for part in range(parts):
                if len(pieces) == 1:
                    arrived[part].append((group, part))
                elif p == part:
                    arrived[part].append((group, 0))
        base += made

    per_kind, blocks = coupling_tables(
        growth, whitecap, weights, spread, cosine, sine, sent[0], lon
    )

    returned = []
    for part in range(parts):
        made = couple(
            assignment, arrived[part], land_mask, wind_field, per_kind, blocks,
            count, comps_dev, part,
        )
        returned.append(swap(made, count))
    order = order_of(count)
    out = None
    for part in range(parts):
        stages = [[0] + order] if part < parts - 1 else stages_of(count)
        for ks in stages:
            out = settle(returned[part], ks, part, rows_dev, lat, out)
    return out


def solution(mesh):
    in_specs = (
        P("group", None, "sector"),
        P(None, "sector"),
        P(None, "group", "sector"),
        P(),
        P(),
        P(),
        P(),
        P(),
        P(),
    )
    out_specs = P("group", None, "sector")
    return jax.shard_map(local, mesh=mesh, in_specs=in_specs, out_specs=out_specs, check_vma=False)
```

```python
import math

import jax
import jax.numpy as jnp
import numpy as np
from jax import lax
from jax.experimental import pallas as pl
from jax.experimental.pallas import tpu as pltpu
from jax.sharding import PartitionSpec as P


DIRS = 36
SUBSTEPS = 6
EDGE = 8
ROWS = 8
UNITS = 24
CHUNKS = (7, 7, 10)
STRIP_BLOCKS = 4
STREAMS = 5
BAND = 4
PAD = 8
LANES = 6


def strip_blocks(base, made, most):
    for block in range(most, 0, -1):
        for streams in range(STREAMS, 0, -1):
            part = block // streams
            if made % block == 0 and block % streams == 0 and base % part == 0:
                return block, streams


def edge_strips(spectrum, land_mask, base, made, most):
    _, lat, lon = spectrum.shape
    block, copies = strip_blocks(base, made, most)
    part = block // copies

    def kernel(*rest):
        waves, (land_ref, near_ref, far_ref, turned) = rest[:copies], rest[copies:]
        step = pl.program_id(0)
        even = lax.rem(lax.axis_index("sector"), 2) == 0
        near = jnp.where(even, lon - SUBSTEPS, 0)
        far = jnp.where(even, 0, lon - SUBSTEPS)
        for b in range(block):
            turned[b] = waves[b // part][b % part].T
            spot = pl.ds((step * block + b) * SUBSTEPS, SUBSTEPS)
            near_ref[spot] = turned[b, pl.ds(near, SUBSTEPS)]
            far_ref[spot] = turned[b, pl.ds(far, SUBSTEPS)]

        @pl.when(step == 0)
        def _():
            turned[0] = land_ref[...].astype(jnp.float32).T
            near_ref[made * SUBSTEPS :] = turned[0, pl.ds(near, SUBSTEPS)]
            far_ref[made * SUBSTEPS :] = turned[0, pl.ds(far, SUBSTEPS)]

    strip = pl.BlockSpec(((made + 1) * SUBSTEPS, lat), lambda i, *_: (0, 0))
    shape = jax.ShapeDtypeStruct(((made + 1) * SUBSTEPS, lat), jnp.float32)
    first = base // part
    streams = [
        pl.BlockSpec((part, lat, lon), lambda i, *_, n=n: (first + i * copies + n, 0, 0))
        for n in range(copies)
    ]
    return pl.pallas_call(
        kernel,
        grid=(made // block,),
        in_specs=streams + [pl.BlockSpec((lat, lon), lambda i: (0, 0))],
        out_specs=[strip, strip],
        scratch_shapes=[pltpu.VMEM((block, lon, lat), jnp.float32)],
        out_shape=[shape, shape],
        cost_estimate=pl.CostEstimate(
            flops=0, bytes_accessed=8 * made * lat * lon, transcendentals=0
        ),
        name="edge_strips",
    )(*[spectrum] * copies, land_mask)


def advance(tables, spectrum, strips, land_mask, inverse, base, made, block, count, pieces):
    comps_dev, lat, lon = spectrum.shape
    rows_dev = sum(pieces)
    span = lon + EDGE
    lanes = LANES if block % LANES == 0 else 3 if block % 3 == 0 else 1

    def kernel(
        kinds_ref, courant_ref, cos_ref, sin_ref,
        wave_ref, near_ref, far_ref, land_ref, inverse_ref,
        *rest,
    ):
        outs, rest = rest[: len(pieces) * count], rest[len(pieces) * count :]
        sea, slope, side = rest[:3]
        sets = [rest[3 + 6 * q : 9 + 6 * q] for q in range(lanes)]
        step = pl.program_id(0)
        me = lax.axis_index("group")
        even = lax.rem(lax.axis_index("sector"), 2) == 0

        @pl.when(step == 0)
        def _():
            for ping, pong, *_ in sets:
                ping[...] = jnp.zeros_like(ping)
                pong[...] = jnp.zeros_like(pong)
            own = land_ref[...].astype(jnp.float32).T
            sea[0, EDGE:] = own
            sea[1, :lon] = own
            sea[0, :EDGE] = jnp.zeros((EDGE, lat), jnp.float32)
            sea[1, lon:] = jnp.zeros((EDGE, lat), jnp.float32)
            near_sea, far_sea = near_ref[made * SUBSTEPS :], far_ref[made * SUBSTEPS :]
            sea[0, EDGE - SUBSTEPS : EDGE] = jnp.where(even, far_sea, near_sea)
            sea[1, lon : lon + SUBSTEPS] = jnp.where(even, near_sea, far_sea)
            lane = lax.broadcasted_iota(jnp.int32, (span, lat), 1)
            for way in range(2):
                slope[way] = sea[way] * inverse_ref[...]
                side[way] = jnp.where(lane == 0, 0.0, sea[way])
                side[2 + way] = jnp.where(lane == lat - 1, 0.0, sea[way])

        def some(i, carry):
            easts, turns = [], []
            for q, (ping, pong, keep, cross, along, result) in enumerate(sets):
                b = i * lanes + q
                kind = kinds_ref[me * comps_dev + base + step * block + b]
                speed = courant_ref[lax.div(kind, DIRS)]
                flow_x = speed * cos_ref[lax.rem(kind, DIRS)]
                flow_y = speed * sin_ref[lax.rem(kind, DIRS)]
                eastward = flow_x > 0.0
                northward = flow_y > 0.0
                way = jnp.where(eastward, 0, 1)
                easts.append(jnp.full((EDGE, lat), way) == 0)
                turns.append(jnp.where(northward, 1, lat - 1))
                rate_x, rate_y = jnp.abs(flow_x), jnp.abs(flow_y)
                ratio = rate_x * slope[way]
                cross[...] = ratio
                along[...] = rate_y * side[jnp.where(northward, way, 2 + way)]
                keep[...] = (1.0 - rate_y) * sea[way] - ratio
                own = pl.multiple_of(jnp.where(eastward, 2 * EDGE, EDGE), EDGE)
                upwind = jnp.where(eastward, 2 * EDGE - SUBSTEPS, EDGE + lon)
                ping[pl.ds(own, lon)] = wave_ref[b].T
                spot = pl.ds((step * block + b) * SUBSTEPS, SUBSTEPS)
                ping[pl.ds(upwind, SUBSTEPS)] = jnp.where(
                    eastward == even, far_ref[spot], near_ref[spot]
                )
            for substep in range(SUBSTEPS):
                for row in range(0, span, EDGE):
                    for q, (ping, pong, keep, cross, along, result) in enumerate(sets):
                        now, then = (ping, pong) if substep % 2 == 0 else (pong, ping)
                        spot = slice(row, row + EDGE)
                        here = now[row + EDGE : row + 2 * EDGE]
                        upwind = jnp.where(
                            easts[q],
                            now[row + EDGE - 1 : row + 2 * EDGE - 1],
                            now[row + EDGE + 1 : row + 2 * EDGE + 1],
                        )
                        then[row + EDGE : row + 2 * EDGE] = (
                            keep[spot] * here
                            + cross[spot] * upwind
                            + along[spot] * pltpu.roll(here, turns[q], 1)
                        )
            for q, (ping, pong, keep, cross, along, result) in enumerate(sets):
                b = i * lanes + q
                last = ping if SUBSTEPS % 2 == 0 else pong
                kind = kinds_ref[me * comps_dev + base + step * block + b]
                eastward = cos_ref[lax.rem(kind, DIRS)] > 0.0
                own = pl.multiple_of(jnp.where(eastward, 2 * EDGE, EDGE), EDGE)
                result[...] = last[pl.ds(own, lon)].T
                offset = 0
                for p, rows in enumerate(pieces):
                    for k in range(count):
                        row = pl.multiple_of((me ^ k) * rows_dev + offset, ROWS)
                        outs[p * count + k][b] = result[pl.ds(row, rows)]
                    offset += rows
            return carry

        lax.fori_loop(0, block // lanes, some, 0)

    fixed = lambda shape: pl.BlockSpec(shape, lambda i, *_: (0,) * len(shape))
    first_block = base // block
    f32 = lambda *shape: pltpu.VMEM(shape, jnp.float32)
    return pl.pallas_call(
        kernel,
        grid_spec=pltpu.PrefetchScalarGridSpec(
            num_scalar_prefetch=4,
            grid=(made // block,),
            in_specs=[
                pl.BlockSpec((block, lat, lon), lambda i, *_: (first_block + i, 0, 0)),
                fixed(((made + 1) * SUBSTEPS, lat)),
                fixed(((made + 1) * SUBSTEPS, lat)),
                fixed((lat, lon)),
                fixed((1, lat)),
            ],
            out_specs=[
                pl.BlockSpec((block, rows, lon), lambda i, *_: (i, 0, 0))
                for rows in pieces
                for _ in range(count)
            ],
            scratch_shapes=[f32(2, span, lat), f32(2, span, lat), f32(4, span, lat)]
            + [
                f32(span + 2 * EDGE, lat), f32(span + 2 * EDGE, lat),
                f32(span, lat), f32(span, lat), f32(span, lat),
                f32(lat, lon),
            ] * lanes,
        ),
        out_shape=[
            jax.ShapeDtypeStruct((made, rows, lon), jnp.float32)
            for rows in pieces
            for _ in range(count)
        ],
        cost_estimate=pl.CostEstimate(
            flops=0, bytes_accessed=12 * made * lat * lon * 4, transcendentals=0
        ),
        name="advance",
    )(*tables, spectrum, *strips, land_mask, inverse)


def coupling_tables(growth, whitecap, weights, spread, cosine, sine, after, lon):
    freqs, dirs, _ = spread.shape
    comps = freqs * dirs
    bands, band = freqs // BAND, BAND * dirs

    def kernel(growth_ref, decay_ref, weight_ref, spread_ref, cos_ref, sin_ref, _, *rest):
        weights_ref, east_ref, north_ref, decays_ref, high_ref, low_ref, whole = rest
        one = jnp.ones((dirs, lon), jnp.float32)
        for f in range(freqs):
            rows = slice(f * dirs, (f + 1) * dirs)
            weights_ref[rows] = weight_ref[f] * one
            east_ref[rows] = growth_ref[f] * cos_ref[...]
            north_ref[rows] = growth_ref[f] * sin_ref[...]
            decays_ref[rows] = decay_ref[f] * one
        whole[...] = jnp.zeros_like(whole)
        for n in range(bands):
            for q in range(BAND):
                spot = slice(q * dirs, (q + 1) * dirs)
                whole[spot, spot] = 0.5 * spread_ref[n * BAND + q]
            high = whole[...].astype(jnp.bfloat16)
            high_ref[n] = high
            low_ref[n] = (whole[...] - high.astype(jnp.float32)).astype(jnp.bfloat16)

    scalars = pl.BlockSpec(memory_space=pltpu.SMEM)
    vmem = pl.BlockSpec(memory_space=pltpu.VMEM)
    spread_out = lambda values: jnp.asarray(np.repeat(values[:, None], lon, axis=1))
    rates = jax.ShapeDtypeStruct((comps, lon), jnp.float32)
    part = jax.ShapeDtypeStruct((bands, band, band), jnp.bfloat16)
    made = pl.pallas_call(
        kernel,
        in_specs=[scalars] * 3 + [vmem] * 3 + [pl.BlockSpec(memory_space=pl.ANY)],
        out_specs=[vmem] * 6,
        out_shape=[rates] * 4 + [part] * 2,
        scratch_shapes=[pltpu.VMEM((band, band), jnp.float32)],
        cost_estimate=pl.CostEstimate(
            flops=0, bytes_accessed=20 * comps * lon, transcendentals=0
        ),
        name="coupling_tables",
    )(growth, whitecap, weights, spread, spread_out(cosine), spread_out(sine), after)
    return made[:4], made[4:]


def couple(assignment, arrived, land_mask, winds, per_kind, blocks, count, comps_dev, part):
    comps = assignment.shape[0]
    lon = land_mask.shape[1]
    rows_dev = winds.shape[1]
    bands, band, _ = blocks[0].shape
    flat = [a for group, _ in arrived for a in group]
    sizes = [group[0].shape[0] for group, _ in arrived]
    pitch = comps + PAD
    unroll = 8 if all(size % 8 == 0 for size in sizes) else 6

    def kernel(kinds_ref, *rest):
        ins, rest = rest[: len(flat)], rest[len(flat) :]
        land_ref, wind_ref, weight_ref, east_ref, north_ref, decay_ref, high_ref, low_ref = rest[:8]
        outs, (sorted_ref,) = rest[8:-1], rest[-1:]
        me = lax.axis_index("group")
        for k in range(count):
            for g in range(len(arrived)):
                first = (me ^ k) * comps_dev + sum(sizes[:g])
                source = ins[g * count + k]

                def put(i, carry, source=source, first=first):
                    rows = [i * unroll + u for u in range(unroll)]
                    kinds = [kinds_ref[first + c] for c in rows]
                    values = [source[c] for c in rows]
                    for kind, value in zip(kinds, values):
                        sorted_ref[pl.ds(kind, ROWS, stride=pitch), :] = value
                    return carry

                lax.fori_loop(0, sizes[g] // unroll, put, 0)

        def pair(p, carry):
            starts = [pl.multiple_of((2 * p + q) * pitch, 8) for q in range(2)]
            loads, us, vs, seas = [], [], [], []
            for q in range(2):
                j = 2 * p + q
                total = jnp.sum(
                    weight_ref[...] * sorted_ref[pl.ds(starts[q], comps), :], axis=0, keepdims=True
                )
                loading = total / comps
                loads.append(loading / (1.0 + loading))
                us.append(wind_ref[0, pl.ds(j, 1), :])
                vs.append(wind_ref[1, pl.ds(j, 1), :])
                sea_row = land_ref[pl.ds(me * rows_dev + part * ROWS + j, 1), :]
                seas.append(sea_row.astype(jnp.float32))
            for n in range(bands):
                kinds = slice(n * band, (n + 1) * band)
                spots = [pl.ds(pl.multiple_of(starts[q] + n * band, 8), band) for q in range(2)]
                energy = [sorted_ref[spots[q], :] for q in range(2)]
                both = jnp.concatenate(energy, axis=1)
                high = both.astype(jnp.bfloat16)
                low = (both - high.astype(jnp.float32)).astype(jnp.bfloat16)
                dot = lambda a, b: jnp.dot(a, b, preferred_element_type=jnp.float32)
                mixed = dot(high_ref[n], high) + (dot(high_ref[n], low) + dot(low_ref[n], high))
                for q in range(2):
                    drive = east_ref[kinds, :] * us[q] + north_ref[kinds, :] * vs[q]
                    exponent = jnp.maximum(drive, 0.0) - decay_ref[kinds, :] * loads[q]
                    sorted_ref[spots[q], :] = seas[q] * (
                        energy[q] * jnp.exp(exponent) + mixed[:, q * lon : (q + 1) * lon]
                    )
            return carry

        lax.fori_loop(0, ROWS // 2, pair, 0)
        step = 8 if comps_dev % 8 == 0 else 6
        for k in range(count):

            def take(i, carry, k=k):
                rows = [i * step + u for u in range(step)]
                kinds = [kinds_ref[(me ^ k) * comps_dev + c] for c in rows]
                values = [sorted_ref[pl.ds(kind, ROWS, stride=pitch), :] for kind in kinds]
                for c, value in zip(rows, values):
                    outs[k][c] = value
                return carry

            lax.fori_loop(0, comps_dev // step, take, 0)

    vmem = pl.BlockSpec(memory_space=pltpu.VMEM)
    pieces = [
        pl.BlockSpec((a.shape[0], ROWS, lon), lambda *_, at=at: (0, at, 0))
        for group, at in arrived
        for a in group
    ]
    wind_rows = pl.BlockSpec((2, ROWS, lon), lambda *_: (0, part, 0))
    return pl.pallas_call(
        kernel,
        grid_spec=pltpu.PrefetchScalarGridSpec(
            num_scalar_prefetch=1,
            grid=(1,),
            in_specs=pieces + [vmem, wind_rows] + [vmem] * 6,
            out_specs=[vmem] * count,
            scratch_shapes=[pltpu.VMEM((ROWS * pitch, lon), jnp.float32)],
        ),
        out_shape=[jax.ShapeDtypeStruct((comps_dev, ROWS, lon), jnp.float32)] * count,
        cost_estimate=pl.CostEstimate(
            flops=0, bytes_accessed=8 * comps * ROWS * lon * 4, transcendentals=0
        ),
        name="couple",
    )(assignment, *flat, land_mask, winds, *per_kind, *blocks)


def settle(returned, ks, part, rows_dev, lat, partial):
    comps_dev, _, lon = returned[0].shape
    cuts = 4 if len(ks) <= 2 else 2
    cut = comps_dev // cuts
    jobs = [(n, k, c) for n, k in enumerate(ks) for c in range(cuts)]
    amount = len(jobs)

    def kernel(*rest):
        ins, out_ref, (held, in_sem, out_sem) = rest[: len(ks)], rest[-4], rest[-3:]
        me = lax.axis_index("group")
        into, out = [], []
        for job, (n, k, c) in enumerate(jobs):
            row = pl.multiple_of((me ^ k) * rows_dev + part * ROWS, ROWS)
            some = pl.ds(c * cut, cut)
            into.append(pltpu.make_async_copy(ins[n].at[some], held.at[job], in_sem.at[job]))
            target = out_ref.at[some, pl.ds(row, ROWS), :]
            out.append(pltpu.make_async_copy(held.at[job], target, out_sem.at[job]))
        for copy in into:
            copy.start()
        for job in range(amount):
            into[job].wait()
            out[job].start()
        for copy in out:
            copy.wait()

    anywhere = pl.BlockSpec(memory_space=pl.ANY)
    extra = [] if partial is None else [partial]
    return pl.pallas_call(
        kernel,
        in_specs=[anywhere] * (len(ks) + len(extra)),
        out_specs=anywhere,
        scratch_shapes=[
            pltpu.VMEM((amount, cut, ROWS, lon), jnp.float32),
            pltpu.SemaphoreType.DMA((amount,)),
            pltpu.SemaphoreType.DMA((amount,)),
        ],
        out_shape=jax.ShapeDtypeStruct((comps_dev, lat, lon), jnp.float32),
        input_output_aliases={len(ks): 0} if extra else {},
        cost_estimate=pl.CostEstimate(
            flops=0, bytes_accessed=2 * len(ks) * comps_dev * ROWS * lon * 4, transcendentals=0
        ),
        name="settle",
    )(*[returned[k] for k in ks], *extra)


def order_of(count):
    return [k for k in (*range(2, count, 2), *range(3, count, 2))] + [1]


def stages_of(count):
    order = order_of(count)
    return [[0, 1] + order[: count - 5], order[count - 5 : count - 4], order[count - 4 : count - 2]]


def swap(pieces, count):
    made = [pieces[0]] + [None] * (count - 1)
    for k in order_of(count):
        made[k] = lax.ppermute(pieces[k], "group", [(i, i ^ k) for i in range(count)])
    return made


def exchange(near, far):
    count = lax.axis_size("sector")
    pairs = [(i, i ^ 1) for i in range(count)]
    near = lax.ppermute(near, "sector", pairs)
    pairs = [(i, (i + 1) % count if i % 2 else (i - 1) % count) for i in range(count)]
    far = lax.ppermute(far, "sector", pairs)
    return near, far


def local(spectrum, land_mask, wind_field, assignment, courant, growth, whitecap, weights, spread):
    count = lax.axis_size("group")
    comps_dev, lat, lon = spectrum.shape
    rows_dev = wind_field.shape[1]
    parts = rows_dev // ROWS
    unit = comps_dev // UNITS

    angles = (np.arange(DIRS) + 0.5) * (2.0 * math.pi / DIRS)
    cosine, sine = np.float32(np.cos(angles)), np.float32(np.sin(angles))
    latitude = (np.arange(lat) + 0.5 - lat / 2) * (math.pi / 2160.0)
    inverse = jnp.asarray(1.0 / np.cos(latitude), jnp.float32)[None, :]
    tables = (assignment, courant, jnp.asarray(cosine), jnp.asarray(sine))

    arrived = [[] for _ in range(parts)]
    base = 0
    for c, units in enumerate(CHUNKS):
        made = units * unit
        near, far = edge_strips(
            spectrum, land_mask, base, made, comps_dev // STRIP_BLOCKS
        )
        strips = exchange(near, far)
        pieces = [ROWS] * parts if c == len(CHUNKS) - 1 else [rows_dev]
        sent = advance(
            tables, spectrum, strips, land_mask, inverse, base, made, unit, count, pieces
        )
        for p in range(len(pieces)):
            group = swap(sent[p * count : (p + 1) * count], count)
            for part in range(parts):
                if len(pieces) == 1:
                    arrived[part].append((group, part))
                elif p == part:
                    arrived[part].append((group, 0))
        base += made

    per_kind, blocks = coupling_tables(
        growth, whitecap, weights, spread, cosine, sine, sent[0], lon
    )

    returned = []
    for part in range(parts):
        made = couple(
            assignment, arrived[part], land_mask, wind_field, per_kind, blocks,
            count, comps_dev, part,
        )
        returned.append(swap(made, count))
    order = order_of(count)
    out = None
    for part in range(parts):
        stages = [[0] + order] if part < parts - 1 else stages_of(count)
        for ks in stages:
            out = settle(returned[part], ks, part, rows_dev, lat, out)
    return out


def solution(mesh):
    in_specs = (
        P("group", None, "sector"),
        P(None, "sector"),
        P(None, "group", "sector"),
        P(),
        P(),
        P(),
        P(),
        P(),
        P(),
    )
    out_specs = P("group", None, "sector")
    return jax.shard_map(local, mesh=mesh, in_specs=in_specs, out_specs=out_specs, check_vma=False)
```
